256 devices in a mesh: lat: 16 (over y_hi, z), orient: 16 (over y_lo, x, core).
Axes of the slice: x: 4, y: 4 (y_hi: 2, y_lo: 2; y = y_hi * 2 + y_lo), z: 8, core: 2. Of those that a mesh axis runs over, the one named last changes fastest.
Arguments:
- features: bfloat16 [16, 32, 64, 8192], P('orient', None, 'lat'), may hold values from -6 to 6
- mix_weights: bfloat16 [2, 3, 32, 32], replicated, may hold values from -0.625 to 0.625
- kernels: bfloat16 [2, 9, 32, 32], replicated, may hold values from -0.375 to 0.375
- bias_terms: float32 [2, 32], replicated, may hold values from -3 to 3
Outputs:
- responses: bfloat16 [16, 32, 64, 8192], P('orient', None, 'lat')
The draws below stay inside these ranges and needn't reach their ends.
All inputs are finite; a program needn't handle non-finite values.
Results may differ from the reference program's by a relative error of at most 0.0061.
Values may be sent and summed in bfloat16 or wider, within the bound.
A program may use at most 128 MiB of HBM per device.

```python
import jax
import jax.numpy as jnp
import numpy as np
from jax import lax

ORIENTS = 16
C = 32
W = 8192
LAYERS = 2
ROWS = 64


def steps_of(stream_key, shape, split, smallest, top_value):
    loudness, own = 1.0, jax.random.fold_in(stream_key, 6)
    for dim, parts in split:
        steps = jnp.exp(jax.random.uniform(jax.random.fold_in(own, dim), (parts,), jnp.float32, smallest / len(split), top_value / len(split)))
        loudness = loudness * jnp.repeat(steps, shape[dim] // parts).reshape([-1 if axis == dim else 1 for axis in range(len(shape))])
    return loudness


def scatter_about(stream_key, dims, scale, most, split=(), held_as=jnp.bfloat16):
    loudness = steps_of(stream_key, dims, split, -0.22, 0.18) if split else 1.0
    values = jax.random.normal(stream_key, dims, jnp.float32) * scale * loudness
    return jnp.minimum(jnp.maximum(values, -most), most).astype(held_as)


def setup_inputs(seed: int = 0) -> dict:
    splits = jax.random.split(jax.random.key(seed), 5)
    features = scatter_about(splits[0], (ORIENTS, C, ROWS, W), 1.0, 6.0, ((0, 16), (2, 16)))
    mix_weights = scatter_about(splits[1], (LAYERS, 3, C, C), (3 * C) ** -0.5, 0.625)
    kernels = scatter_about(splits[2], (LAYERS, 9, C, C), (9 * C) ** -0.5, 0.375)
    bias_terms = scatter_about(splits[3], (LAYERS, C), 0.5, 3.0, (), jnp.float32)
    return {"features": features, "mix_weights": mix_weights, "kernels": kernels, "bias_terms": bias_terms}


CYCLE_PLACE = np.array([0, 1, 2, 7, -1, 3, 6, 5, 4])
CYCLE_PAIRS = np.outer((CYCLE_PLACE >= 0).astype(np.float32), (CYCLE_PLACE >= 0).astype(np.float32))
CENTER_ONE = np.outer((CYCLE_PLACE < 0).astype(np.float32), (CYCLE_PLACE < 0).astype(np.float32))


def rotation_table(orient):
    half_turn = orient.astype(jnp.float32) * 0.5
    positions = jnp.asarray(CYCLE_PLACE).astype(jnp.float32)
    distance = jnp.mod(positions[:, None] - positions[None, :] - half_turn + 4.0, 8.0) - 4.0
    weight = jnp.maximum(0.0, 1.0 - jnp.abs(distance))
    return weight * jnp.asarray(CYCLE_PAIRS).astype(jnp.float32) + jnp.asarray(CENTER_ONE).astype(jnp.float32)


def rotated_kernels(kernel, orient):
    table = rotation_table(orient)
    return jnp.einsum("ab,bij->aij", table, kernel.astype(jnp.float32), precision=lax.Precision.HIGHEST).astype(jnp.bfloat16)


def one_layer(current, mixing, kernel, bias_row):
    def per_orient(orient):
        running = jnp.zeros((C, ROWS, W), jnp.float32)
        for offset in range(3):
            source = current[jnp.mod(orient + offset - 1, ORIENTS)]
            running = running + jnp.einsum("ij,jrw->irw", mixing[offset].astype(jnp.float32), source.astype(jnp.float32))
        mixed_feats = running.astype(jnp.bfloat16)
        padded = jnp.pad(mixed_feats, ((0, 0), (1, 1), (0, 0)))
        rotated = rotated_kernels(kernel, orient)
        result = jnp.zeros((C, ROWS, W), jnp.float32)
        for tap_index in range(9):
            row_start = tap_index // 3
            col_shift = tap_index % 3 - 1
            window = jnp.roll(padded[:, row_start:row_start + ROWS, :], -col_shift, axis=2)
            result = result + jnp.einsum("ij,jrw->irw", rotated[tap_index].astype(jnp.float32), window.astype(jnp.float32))
        return jax.nn.relu(result + bias_row[:, None, None]).astype(jnp.bfloat16)

    return lax.map(per_orient, jnp.arange(ORIENTS, dtype=jnp.int32))


def reference(features, mix_weights, kernels, bias_terms):
    current = features
    for layer_index in range(LAYERS):
        current = one_layer(current, mix_weights[layer_index], kernels[layer_index], bias_terms[layer_index])
    return current
```

```python
import functools

import jax
import jax.numpy as jnp
from jax import lax
from jax.experimental import pallas as pl
from jax.experimental.pallas import tpu as pltpu
from jax.sharding import PartitionSpec as P

LAYERS = 2
C = 32
MESH = pl.DeviceIdType.MESH
CHUNKS = 16
LAG = 2
CYCLE_TAPS = (0, 1, 2, 5, 8, 7, 6, 3)
BF = jnp.bfloat16
F32 = jnp.float32


def iota(shape, dim):
    return lax.broadcasted_iota(jnp.int32, shape, dim)


def one_hot(cond):
    return jnp.where(cond, 1.0, 0.0).astype(BF)


def build_mix(a_ref, w_ref, layer, rows, natural):
    depth = rows * C
    lane, chan = iota((C, depth), 1), iota((C, depth), 0)
    for r in range(rows):
        place = chan * rows + r if natural else chan + r * C
        pick = one_hot(lane == place)
        for k in range(3):
            block = jnp.dot(w_ref[layer, k], pick, preferred_element_type=F32)
            a_ref[r * C : (r + 1) * C, k * depth : (k + 1) * depth] = block.astype(BF)


def build_conv(c_ref, kern_ref, cyc_ref, layer, rows, orient, natural):
    depth = (rows + 2) * C
    for p, tap in enumerate(CYCLE_TAPS):
        cyc_ref[p] = kern_ref[layer, tap].astype(F32)
    low = orient // 2
    high = (orient + 1) // 2
    lane, chan = iota((C, depth), 1), iota((C, depth), 0)
    for dx in range(3):
        for r in range(rows):
            total = jnp.zeros((C, depth), F32)
            for dy in range(3):
                tap = 3 * dy + dx
                if tap == 4:
                    rot = kern_ref[layer, 4]
                else:
                    p = CYCLE_TAPS.index(tap)
                    first = cyc_ref[(p + 16 - low) % 8]
                    second = cyc_ref[(p + 16 - high) % 8]
                    rot = (0.5 * first + 0.5 * second).astype(BF)
                source = r + dy - 1
                if source < 0:
                    base = rows * C
                elif source >= rows:
                    base = (rows + 1) * C
                else:
                    base = source * C
                pick = one_hot(lane == chan + base)
                total = total + jnp.dot(rot, pick, preferred_element_type=F32)
            c_ref[r * C : (r + 1) * C, dx * depth : (dx + 1) * depth] = total.astype(BF)
    if natural:
        out, src = iota((rows * C, rows * C), 0), iota((rows * C, rows * C), 1)
        order = one_hot(out == (src % C) * rows + src // C)
        c_ref[...] = jnp.dot(order, c_ref[...], preferred_element_type=F32).astype(BF)


def build_bias(b_ref, bias_ref, layer, rows, natural):
    row, chan = iota((rows * C, C), 0), iota((rows * C, C), 1)
    place = row // rows if natural else row % C
    spread = jnp.where(place == chan, bias_ref[layer : layer + 1, :], 0.0)
    column = jnp.sum(spread, axis=1, keepdims=True)
    b_ref[layer] = jnp.broadcast_to(column, (rows * C, 128))


def kernel(
    orients,
    lats,
    x_hbm,
    w_hbm,
    k_hbm,
    bias_hbm,
    out_ref,
    own,
    left0,
    right0,
    left1,
    right1,
    mixed0,
    mixed1,
    top0,
    top1,
    bottom0,
    bottom1,
    current1,
    result,
    w_ref,
    k_ref,
    bias_ref,
    cyc,
    a0,
    a1,
    c0,
    c1,
    b_ref,
    local_sem,
    left_send,
    left_recv,
    right_send,
    right_recv,
    up_send,
    up_recv,
    down_send,
    down_recv,
    out_sem,
):
    rows, width = x_hbm.shape[2], x_hbm.shape[3]
    n = CHUNKS
    size = width // n
    edge = 128
    depth = rows * C
    orient = lax.axis_index("orient")
    lat = lax.axis_index("lat")
    right = {"orient": lax.rem(orient + 1, orients)}
    left = {"orient": lax.rem(orient + orients - 1, orients)}
    above = {"lat": lat - 1}
    below = {"lat": lat + 1}
    has_above = lat > 0
    has_below = lat < lats - 1

    def lanes(chunk):
        return pl.ds(pl.multiple_of(chunk * size, size), size)

    def remote(src, dst, send, recv, device):
        return pltpu.make_async_remote_copy(
            src_ref=src, dst_ref=dst, send_sem=send, recv_sem=recv, device_id=device, device_id_type=MESH
        )

    barrier = pltpu.get_barrier_semaphore()
    pl.semaphore_signal(barrier, inc=1, device_id=left, device_id_type=MESH)
    pl.semaphore_signal(barrier, inc=1, device_id=right, device_id_type=MESH)

    @pl.when(has_above)
    def _():
        pl.semaphore_signal(barrier, inc=1, device_id=above, device_id_type=MESH)

    @pl.when(has_below)
    def _():
        pl.semaphore_signal(barrier, inc=1, device_id=below, device_id_type=MESH)

    local = [
        pltpu.make_async_copy(w_hbm, w_ref, local_sem.at[0]),
        pltpu.make_async_copy(k_hbm, k_ref, local_sem.at[1]),
        pltpu.make_async_copy(bias_hbm, bias_ref, local_sem.at[2]),
        pltpu.make_async_copy(x_hbm.at[0], own, local_sem.at[3]),
    ]
    for copy in local:
        copy.start()

    peers = 2 + jnp.where(has_above, 1, 0) + jnp.where(has_below, 1, 0)
    pl.semaphore_wait(barrier, peers)

    def orient_copies(layer, chunk):
        s = lanes(chunk)
        if layer == 0:
            src, to_left, to_right = x_hbm.at[0, :, :, s], right0.at[:, :, s], left0.at[:, :, s]
        else:
            src, to_left, to_right = current1.at[:, s], right1.at[:, s], left1.at[:, s]
        return (
            remote(src, to_left, left_send.at[layer, chunk], left_recv.at[layer, chunk], left),
            remote(src, to_right, right_send.at[layer, chunk], right_recv.at[layer, chunk], right),
        )

    def lat_copies(layer, chunk):
        s = lanes(chunk)
        mixed, top, bottom = ((mixed0, top0, bottom0), (mixed1, top1, bottom1))[layer]
        return (
            remote(mixed.at[0:C, s], bottom.at[:, s], up_send.at[layer, chunk], up_recv.at[layer, chunk], above),
            remote(
                mixed.at[depth - C : depth, s], top.at[:, s], down_send.at[layer, chunk], down_recv.at[layer, chunk], below
            ),
        )

    @pl.loop(0, n)
    def _(chunk):
        for copy in orient_copies(0, chunk):
            copy.start()

    @pl.when(jnp.logical_not(has_above))
    def _():
        top0[...] = jnp.zeros_like(top0)
        top1[...] = jnp.zeros_like(top1)

    @pl.when(jnp.logical_not(has_below))
    def _():
        bottom0[...] = jnp.zeros_like(bottom0)
        bottom1[...] = jnp.zeros_like(bottom1)

    for copy in local:
        copy.wait()
    build_mix(a0, w_ref, 0, rows, True)
    build_mix(a1, w_ref, 1, rows, False)
    build_conv(c0, k_ref, cyc, 0, rows, orient, False)
    build_conv(c1, k_ref, cyc, 1, rows, orient, True)
    build_bias(b_ref, bias_ref, 0, rows, False)
    build_bias(b_ref, bias_ref, 1, rows, True)

    def mix(layer, chunk):
        s = lanes(chunk)
        if layer == 0:
            parts = [ref[:, :, s].reshape(depth, size) for ref in (left0, own, right0)]
        else:
            parts = [ref[:, s] for ref in (left1, current1, right1)]
        weights, mixed = ((a0, mixed0), (a1, mixed1))[layer]
        total = jnp.dot(weights[...], jnp.concatenate(parts, axis=0), preferred_element_type=F32)
        mixed[:, s] = total.astype(BF)

    def conv(layer, chunk):
        mixed, top, bottom, weights = ((mixed0, top0, bottom0, c0), (mixed1, top1, bottom1, c1))[layer]
        before = pl.ds(pl.multiple_of(lax.rem(chunk * size + width - edge, width), edge), edge)
        after = pl.ds(pl.multiple_of(lax.rem(chunk * size + size, width), edge), edge)

        def part(s):
            return jnp.concatenate([mixed[:, s], top[:, s], bottom[:, s]], axis=0)

        middle = part(lanes(chunk))
        wide = jnp.concatenate([part(before), middle, part(after)], axis=1)
        whole = size + 2 * edge
        west = pltpu.roll(wide, 1, 1)[:, edge : edge + size]
        east = pltpu.roll(wide, whole - 1, 1)[:, edge : edge + size]
        total = jnp.dot(weights[...], jnp.concatenate([west, middle, east], axis=0), preferred_element_type=F32)
        bias = jnp.tile(b_ref[layer], (1, size // 128))
        return jnp.maximum(total + bias, 0.0).astype(BF)

    for layer in range(LAYERS):

        @pl.loop(0, n + 2 + LAG)
        def _(step, layer=layer):
            @pl.when(step < n)
            def _():
                chunk = lax.rem(step + layer, n)
                for copy in orient_copies(layer, chunk):
                    copy.wait_recv()
                mix(layer, chunk)
                up, down = lat_copies(layer, chunk)

                @pl.when(has_above)
                def _():
                    up.start()

                @pl.when(has_below)
                def _():
                    down.start()

            @pl.when(jnp.logical_and(step >= LAG, step < n + LAG))
            def _():
                chunk = lax.rem(step - LAG + layer, n)
                up, down = lat_copies(layer, chunk)

                @pl.when(has_below)
                def _():
                    up.wait_recv()

                @pl.when(has_above)
                def _():
                    down.wait_recv()

            @pl.when(step >= LAG + 2)
            def _():
                chunk = lax.rem(step - LAG - 1 + layer, n)
                values = conv(layer, chunk)
                s = lanes(chunk)
                if layer == 0:
                    current1[:, s] = values
                    for copy in orient_copies(1, chunk):
                        copy.start()
                else:
                    result[:, :, s] = values.reshape(C, rows, size)
                    pltpu.make_async_copy(result.at[:, :, s], out_ref.at[0, :, :, s], out_sem.at[chunk]).start()

    @pl.loop(0, n)
    def _(chunk):
        s = lanes(chunk)
        pltpu.make_async_copy(result.at[:, :, s], out_ref.at[0, :, :, s], out_sem.at[chunk]).wait()
        for layer in range(LAYERS):
            for copy in orient_copies(layer, chunk):
                copy.wait_send()
            up, down = lat_copies(layer, chunk)

            @pl.when(has_above)
            def _():
                up.wait_send()

            @pl.when(has_below)
            def _():
                down.wait_send()


def solution(mesh):
    orients, lats = mesh.shape["orient"], mesh.shape["lat"]

    def local(features, mix_weights, kernels, bias_terms):
        _, _, rows, width = features.shape
        depth = rows * C
        raw = pltpu.VMEM((C, rows, width), BF)
        flat = pltpu.VMEM((depth, width), BF)
        row = pltpu.VMEM((C, width), BF)
        sems = pltpu.SemaphoreType.DMA((LAYERS, CHUNKS))
        hbm = pl.BlockSpec(memory_space=pltpu.MemorySpace.HBM)
        return pl.pallas_call(
            functools.partial(kernel, orients, lats),
            out_shape=jax.ShapeDtypeStruct(features.shape, BF),
            in_specs=[hbm] * 4,
            out_specs=pl.BlockSpec(memory_space=pl.ANY),
            scratch_shapes=[raw, raw, raw, flat, flat, flat, flat, row, row, row, row, flat, raw]
            + [
                pltpu.VMEM(mix_weights.shape, BF),
                pltpu.VMEM(kernels.shape, BF),
                pltpu.VMEM(bias_terms.shape, F32),
                pltpu.VMEM((8, C, C), F32),
                pltpu.VMEM((depth, 3 * depth), BF),
                pltpu.VMEM((depth, 3 * depth), BF),
                pltpu.VMEM((depth, 3 * (rows + 2) * C), BF),
                pltpu.VMEM((depth, 3 * (rows + 2) * C), BF),
                pltpu.VMEM((LAYERS, depth, 128), F32),
                pltpu.SemaphoreType.DMA((4,)),
            ]
            + [sems] * 8
            + [pltpu.SemaphoreType.DMA((CHUNKS,))],
            compiler_params=pltpu.CompilerParams(
                collective_id=0, has_side_effects=True, vmem_limit_bytes=40 << 20
            ),
        )(features, mix_weights, kernels, bias_terms)

    return jax.shard_map(
        local,
        mesh=mesh,
        in_specs=(P("orient", None, "lat", None), P(), P(), P()),
        out_specs=P("orient", None, "lat", None),
        check_vma=False,
    )
```

```python
import functools

import jax
import jax.numpy as jnp
from jax import lax
from jax.experimental import pallas as pl
from jax.experimental.pallas import tpu as pltpu
from jax.sharding import PartitionSpec as P

LAYERS = 2
C = 32
MESH = pl.DeviceIdType.MESH
CHUNKS = 16
LAG = 4
CYCLE_TAPS = (0, 1, 2, 5, 8, 7, 6, 3)
BF = jnp.bfloat16
F32 = jnp.float32


def iota(shape, dim):
    return lax.broadcasted_iota(jnp.int32, shape, dim)


def one_hot(cond):
    return jnp.where(cond, 1.0, 0.0).astype(BF)


def places(rows):
    order = [0, rows - 1] + list(range(1, rows - 1))
    return [order.index(r) for r in range(rows)]


def build_mix0(a_ref, w_ref, rows):
    depth = rows * C
    lane, chan = iota((C, depth), 1), iota((C, depth), 0)
    for r, at in enumerate(places(rows)):
        pick = one_hot(lane == chan * rows + r)
        for k in range(3):
            block = jnp.dot(w_ref[0, k], pick, preferred_element_type=F32)
            a_ref[at * C : (at + 1) * C, k * depth : (k + 1) * depth] = block.astype(BF)


def build_mix1(a_ref, w_ref):
    depth = 2 * C
    lane, chan = iota((C, depth), 1), iota((C, depth), 0)
    for r in range(2):
        pick = one_hot(lane == chan + r * C)
        for k in range(3):
            block = jnp.dot(w_ref[1, k], pick, preferred_element_type=F32)
            a_ref[r * C : (r + 1) * C, k * depth : (k + 1) * depth] = block.astype(BF)


def build_conv(c_ref, kern_ref, cyc_ref, layer, rows, orient, natural):
    depth = (rows + 2) * C
    at = places(rows)
    for p, tap in enumerate(CYCLE_TAPS):
        cyc_ref[p] = kern_ref[layer, tap].astype(F32)
    low = orient // 2
    high = (orient + 1) // 2
    lane, chan = iota((C, depth), 1), iota((C, depth), 0)
    for dx in range(3):
        for r in range(rows):
            total = jnp.zeros((C, depth), F32)
            for dy in range(3):
                tap = 3 * dy + dx
                if tap == 4:
                    rot = kern_ref[layer, 4]
                else:
                    p = CYCLE_TAPS.index(tap)
                    first = cyc_ref[(p + 16 - low) % 8]
                    second = cyc_ref[(p + 16 - high) % 8]
                    rot = (0.5 * first + 0.5 * second).astype(BF)
                source = r + dy - 1
                if source < 0:
                    base = rows * C
                elif source >= rows:
                    base = (rows + 1) * C
                else:
                    base = at[source] * C
                pick = one_hot(lane == chan + base)
                total = total + jnp.dot(rot, pick, preferred_element_type=F32)
            c_ref[at[r] * C : (at[r] + 1) * C, dx * depth : (dx + 1) * depth] = total.astype(BF)
    if natural:
        out, src = iota((rows * C, rows * C), 0), iota((rows * C, rows * C), 1)
        order = jnp.zeros((rows * C, rows * C), BF)
        for r in range(rows):
            order = order + one_hot((src // C == at[r]) & (out == (src % C) * rows + r))
        c_ref[...] = jnp.dot(order, c_ref[...], preferred_element_type=F32).astype(BF)


def build_bias(b_ref, bias_ref, layer, rows, natural):
    row, chan = iota((rows * C, C), 0), iota((rows * C, C), 1)
    place = row // rows if natural else row % C
    spread = jnp.where(place == chan, bias_ref[layer : layer + 1, :], 0.0)
    column = jnp.sum(spread, axis=1, keepdims=True)
    b_ref[layer] = jnp.broadcast_to(column, (rows * C, 128))


def kernel(
    orients,
    lats,
    x_hbm,
    w_hbm,
    k_hbm,
    bias_hbm,
    out_ref,
    own,
    left0,
    right0,
    left1,
    right1,
    mixed0,
    mixed1,
    top0,
    top1,
    bottom0,
    bottom1,
    current1,
    result,
    w_ref,
    k_ref,
    bias_ref,
    cyc,
    a0,
    a1,
    c0,
    c1,
    b_ref,
    local_sem,
    left_send,
    left_recv,
    right_send,
    right_recv,
    up_send,
    up_recv,
    down_send,
    down_recv,
    out_sem,
):
    rows, width = x_hbm.shape[2], x_hbm.shape[3]
    n = CHUNKS
    size = width // n
    edge = 128
    depth = rows * C
    orient = lax.axis_index("orient")
    lat = lax.axis_index("lat")
    right = {"orient": lax.rem(orient + 1, orients)}
    left = {"orient": lax.rem(orient + orients - 1, orients)}
    above = {"lat": lat - 1}
    below = {"lat": lat + 1}
    has_above = lat > 0
    has_below = lat < lats - 1

    def lanes(chunk):
        return pl.ds(pl.multiple_of(chunk * size, size), size)

    def remote(src, dst, send, recv, device):
        return pltpu.make_async_remote_copy(
            src_ref=src, dst_ref=dst, send_sem=send, recv_sem=recv, device_id=device, device_id_type=MESH
        )

    barrier = pltpu.get_barrier_semaphore()
    pl.semaphore_signal(barrier, inc=1, device_id=left, device_id_type=MESH)
    pl.semaphore_signal(barrier, inc=1, device_id=right, device_id_type=MESH)

    @pl.when(has_above)
    def _():
        pl.semaphore_signal(barrier, inc=1, device_id=above, device_id_type=MESH)

    @pl.when(has_below)
    def _():
        pl.semaphore_signal(barrier, inc=1, device_id=below, device_id_type=MESH)

    local = [
        pltpu.make_async_copy(w_hbm, w_ref, local_sem.at[0]),
        pltpu.make_async_copy(k_hbm, k_ref, local_sem.at[1]),
        pltpu.make_async_copy(bias_hbm, bias_ref, local_sem.at[2]),
        pltpu.make_async_copy(x_hbm.at[0], own, local_sem.at[3]),
    ]
    for copy in local:
        copy.start()

    peers = 2 + jnp.where(has_above, 1, 0) + jnp.where(has_below, 1, 0)
    pl.semaphore_wait(barrier, peers)

    half = 2 * C

    def orient_copies(phase, chunk):
        s = lanes(chunk)
        if phase == 0:
            src, to_left, to_right = x_hbm.at[0, :, :, s], right0.at[:, :, s], left0.at[:, :, s]
        else:
            part = slice(0, half) if phase == 1 else slice(half, depth)
            src, to_left, to_right = current1.at[part, s], right1.at[part, s], left1.at[part, s]
        return (
            remote(src, to_left, left_send.at[phase, chunk], left_recv.at[phase, chunk], left),
            remote(src, to_right, right_send.at[phase, chunk], right_recv.at[phase, chunk], right),
        )

    def lat_copies(layer, chunk):
        s = lanes(chunk)
        mixed, top, bottom = ((mixed0, top0, bottom0), (mixed1, top1, bottom1))[layer]
        return (
            remote(mixed.at[0:C, s], bottom.at[:, s], up_send.at[layer, chunk], up_recv.at[layer, chunk], above),
            remote(
                mixed.at[C:half, s], top.at[:, s], down_send.at[layer, chunk], down_recv.at[layer, chunk], below
            ),
        )

    @pl.loop(0, n)
    def _(chunk):
        for copy in orient_copies(0, chunk):
            copy.start()

    @pl.when(jnp.logical_not(has_above))
    def _():
        top0[...] = jnp.zeros_like(top0)
        top1[...] = jnp.zeros_like(top1)

    @pl.when(jnp.logical_not(has_below))
    def _():
        bottom0[...] = jnp.zeros_like(bottom0)
        bottom1[...] = jnp.zeros_like(bottom1)

    for copy in local:
        copy.wait()
    build_mix0(a0, w_ref, rows)
    build_mix1(a1, w_ref)
    build_conv(c0, k_ref, cyc, 0, rows, orient, False)
    build_conv(c1, k_ref, cyc, 1, rows, orient, True)
    build_bias(b_ref, bias_ref, 0, rows, False)
    build_bias(b_ref, bias_ref, 1, rows, True)

    def mix(phase, chunk):
        s = lanes(chunk)
        if phase == 0:
            parts = [ref[:, :, s].reshape(depth, size) for ref in (left0, own, right0)]
            total = jnp.dot(a0[...], jnp.concatenate(parts, axis=0), preferred_element_type=F32)
            mixed0[:, s] = total.astype(BF)
        else:
            part = slice(0, half) if phase == 1 else slice(half, depth)
            parts = [ref[part, s] for ref in (left1, current1, right1)]
            total = jnp.dot(a1[...], jnp.concatenate(parts, axis=0), preferred_element_type=F32)
            mixed1[part, s] = total.astype(BF)

    def conv(layer, chunk):
        mixed, top, bottom, weights = ((mixed0, top0, bottom0, c0), (mixed1, top1, bottom1, c1))[layer]
        before = pl.ds(pl.multiple_of(lax.rem(chunk * size + width - edge, width), edge), edge)
        after = pl.ds(pl.multiple_of(lax.rem(chunk * size + size, width), edge), edge)

        def part(s):
            return jnp.concatenate([mixed[:, s], top[:, s], bottom[:, s]], axis=0)

        middle = part(lanes(chunk))
        wide = jnp.concatenate([part(before), middle, part(after)], axis=1)
        whole = size + 2 * edge
        west = pltpu.roll(wide, 1, 1)[:, edge : edge + size]
        east = pltpu.roll(wide, whole - 1, 1)[:, edge : edge + size]
        total = jnp.dot(weights[...], jnp.concatenate([west, middle, east], axis=0), preferred_element_type=F32)
        bias = jnp.tile(b_ref[layer], (1, size // 128))
        return jnp.maximum(total + bias, 0.0).astype(BF)

    def take(phase, chunk):
        for copy in orient_copies(phase, chunk):
            copy.wait_recv()
        mix(phase, chunk)

    def send_rows(layer, chunk):
        up, down = lat_copies(layer, chunk)

        @pl.when(has_above)
        def _():
            up.start()

        @pl.when(has_below)
        def _():
            down.start()

    def take_rows(layer, chunk):
        up, down = lat_copies(layer, chunk)

        @pl.when(has_below)
        def _():
            up.wait_recv()

        @pl.when(has_above)
        def _():
            down.wait_recv()

    @pl.loop(0, n + 2 + LAG)
    def _(step):
        @pl.when(step < n)
        def _():
            take(0, step)
            send_rows(0, step)

        @pl.when(jnp.logical_and(step >= LAG, step < n + LAG))
        def _():
            take_rows(0, step - LAG)

        @pl.when(step >= LAG + 2)
        def _():
            chunk = lax.rem(step - LAG - 1, n)
            current1[:, lanes(chunk)] = conv(0, chunk)
            for copy in orient_copies(1, chunk):
                copy.start()

    @pl.loop(0, n)
    def _(step):
        for copy in orient_copies(2, lax.rem(step + 1, n)):
            copy.start()

    @pl.loop(0, n)
    def _(step):
        chunk = lax.rem(step + 1, n)
        take(1, chunk)
        send_rows(1, chunk)

    @pl.loop(0, n + 2)
    def _(step):
        @pl.when(step < n)
        def _():
            chunk = lax.rem(step + 1, n)
            take_rows(1, chunk)
            take(2, chunk)

        @pl.when(step >= 2)
        def _():
            chunk = lax.rem(step, n)
            s = lanes(chunk)
            result[:, :, s] = conv(1, chunk).reshape(C, rows, size)
            pltpu.make_async_copy(result.at[:, :, s], out_ref.at[0, :, :, s], out_sem.at[chunk]).start()

    @pl.loop(0, n)
    def _(chunk):
        s = lanes(chunk)
        pltpu.make_async_copy(result.at[:, :, s], out_ref.at[0, :, :, s], out_sem.at[chunk]).wait()
        for phase in range(3):
            for copy in orient_copies(phase, chunk):
                copy.wait_send()
        for layer in range(LAYERS):
            up, down = lat_copies(layer, chunk)

            @pl.when(has_above)
            def _():
                up.wait_send()

            @pl.when(has_below)
            def _():
                down.wait_send()


def solution(mesh):
    orients, lats = mesh.shape["orient"], mesh.shape["lat"]

    def local(features, mix_weights, kernels, bias_terms):
        _, _, rows, width = features.shape
        depth = rows * C
        raw = pltpu.VMEM((C, rows, width), BF)
        flat = pltpu.VMEM((depth, width), BF)
        row = pltpu.VMEM((C, width), BF)
        sems = [pltpu.SemaphoreType.DMA((LAYERS, CHUNKS))] * 4
        phase_sems = [pltpu.SemaphoreType.DMA((3, CHUNKS))] * 4
        hbm = pl.BlockSpec(memory_space=pltpu.MemorySpace.HBM)
        return pl.pallas_call(
            functools.partial(kernel, orients, lats),
            out_shape=jax.ShapeDtypeStruct(features.shape, BF),
            in_specs=[hbm] * 4,
            out_specs=pl.BlockSpec(memory_space=pl.ANY),
            scratch_shapes=[raw, raw, raw, flat, flat, flat, flat, row, row, row, row, flat, raw]
            + [
                pltpu.VMEM(mix_weights.shape, BF),
                pltpu.VMEM(kernels.shape, BF),
                pltpu.VMEM(bias_terms.shape, F32),
                pltpu.VMEM((8, C, C), F32),
                pltpu.VMEM((depth, 3 * depth), BF),
                pltpu.VMEM((2 * C, 6 * C), BF),
                pltpu.VMEM((depth, 3 * (rows + 2) * C), BF),
                pltpu.VMEM((depth, 3 * (rows + 2) * C), BF),
                pltpu.VMEM((LAYERS, depth, 128), F32),
                pltpu.SemaphoreType.DMA((4,)),
            ]
            + phase_sems
            + sems
            + [pltpu.SemaphoreType.DMA((CHUNKS,))],
            compiler_params=pltpu.CompilerParams(
                collective_id=0, has_side_effects=True, vmem_limit_bytes=40 << 20
            ),
        )(*[pltpu.with_memory_space_constraint(v, pltpu.MemorySpace.HBM) for v in (features, mix_weights, kernels, bias_terms)])

    return jax.shard_map(
        local,
        mesh=mesh,
        in_specs=(P("orient", None, "lat", None), P(), P(), P()),
        out_specs=P("orient", None, "lat", None),
        check_vma=False,
    )
```

```python
import functools

import jax
import jax.numpy as jnp
from jax import lax
from jax.experimental import pallas as pl
from jax.experimental.pallas import tpu as pltpu
from jax.sharding import PartitionSpec as P

LAYERS = 2
C = 32
MESH = pl.DeviceIdType.MESH
CHUNKS = 16
LAG = 6
RELAY_LAG = 3
RELAY_LAG1 = 5
ROUTES = 2
CYCLE_TAPS = (0, 1, 2, 5, 8, 7, 6, 3)
BF = jnp.bfloat16
F32 = jnp.float32


def iota(shape, dim):
    return lax.broadcasted_iota(jnp.int32, shape, dim)


def one_hot(cond):
    return jnp.where(cond, 1.0, 0.0).astype(BF)


def places(rows):
    order = [0, rows - 1] + list(range(1, rows - 1))
    return [order.index(r) for r in range(rows)]


def build_mix0(a_ref, w_ref, rows):
    depth = rows * C
    lane, chan = iota((C, depth), 1), iota((C, depth), 0)
    for r, at in enumerate(places(rows)):
        pick = one_hot(lane == chan * rows + r)
        for k in range(3):
            block = jnp.dot(w_ref[0, k], pick, preferred_element_type=F32)
            a_ref[at * C : (at + 1) * C, k * depth : (k + 1) * depth] = block.astype(BF)


def build_mix1(a_ref, w_ref):
    depth = 2 * C
    lane, chan = iota((C, depth), 1), iota((C, depth), 0)
    for r in range(2):
        pick = one_hot(lane == chan + r * C)
        for k in range(3):
            block = jnp.dot(w_ref[1, k], pick, preferred_element_type=F32)
            a_ref[r * C : (r + 1) * C, k * depth : (k + 1) * depth] = block.astype(BF)


def build_conv(c_ref, kern_ref, cyc_ref, layer, rows, orient, natural):
    depth = (rows + 2) * C
    at = places(rows)
    for p, tap in enumerate(CYCLE_TAPS):
        cyc_ref[p] = kern_ref[layer, tap].astype(F32)
    low = orient // 2
    high = (orient + 1) // 2
    lane, chan = iota((C, depth), 1), iota((C, depth), 0)
    for dx in range(3):
        for r in range(rows):
            total = jnp.zeros((C, depth), F32)
            for dy in range(3):
                tap = 3 * dy + dx
                if tap == 4:
                    rot = kern_ref[layer, 4]
                else:
                    p = CYCLE_TAPS.index(tap)
                    first = cyc_ref[(p + 16 - low) % 8]
                    second = cyc_ref[(p + 16 - high) % 8]
                    rot = (0.5 * first + 0.5 * second).astype(BF)
                source = r + dy - 1
                if source < 0:
                    base = rows * C
                elif source >= rows:
                    base = (rows + 1) * C
                else:
                    base = at[source] * C
                pick = one_hot(lane == chan + base)
                total = total + jnp.dot(rot, pick, preferred_element_type=F32)
            c_ref[at[r] * C : (at[r] + 1) * C, dx * depth : (dx + 1) * depth] = total.astype(BF)
    if natural:
        out, src = iota((rows * C, rows * C), 0), iota((rows * C, rows * C), 1)
        order = jnp.zeros((rows * C, rows * C), BF)
        for r in range(rows):
            order = order + one_hot((src // C == at[r]) & (out == (src % C) * rows + r))
        c_ref[...] = jnp.dot(order, c_ref[...], preferred_element_type=F32).astype(BF)


def build_bias(b_ref, bias_ref, layer, rows, natural):
    row, chan = iota((rows * C, C), 0), iota((rows * C, C), 1)
    place = row // rows if natural else row % C
    spread = jnp.where(place == chan, bias_ref[layer : layer + 1, :], 0.0)
    column = jnp.sum(spread, axis=1, keepdims=True)
    b_ref[layer] = jnp.broadcast_to(column, (rows * C, 128))


def kernel(
    orients,
    lats,
    x_hbm,
    w_hbm,
    k_hbm,
    bias_hbm,
    out_ref,
    own,
    left0,
    right0,
    left1,
    right1,
    mixed0,
    mixed1,
    top0,
    top1,
    bottom0,
    bottom1,
    current1,
    result,
    w_ref,
    k_ref,
    bias_ref,
    cyc,
    a0,
    a1,
    c0,
    c1,
    b_ref,
    local_sem,
    left_send,
    left_recv,
    right_send,
    right_recv,
    up_send,
    up_recv,
    down_send,
    down_recv,
    relay,
    relay_send,
    relay_recv,
    out_sem,
):
    rows, width = x_hbm.shape[2], x_hbm.shape[3]
    n = CHUNKS
    size = width // n
    edge = 128
    depth = rows * C
    orient = lax.axis_index("orient")
    lat = lax.axis_index("lat")
    right = {"orient": lax.rem(orient + 1, orients)}
    left = {"orient": lax.rem(orient + orients - 1, orients)}
    above = {"lat": lat - 1}
    below = {"lat": lat + 1}
    has_above = lat > 0
    has_below = lat < lats - 1

    def lanes(chunk):
        return pl.ds(pl.multiple_of(chunk * size, size), size)

    def remote(src, dst, send, recv, device):
        return pltpu.make_async_remote_copy(
            src_ref=src, dst_ref=dst, send_sem=send, recv_sem=recv, device_id=device, device_id_type=MESH
        )

    planes = lats // 2

    place = lax.rem(orient // 2, orients // 4)
    wrapped = jnp.logical_or(place == 0, place == orients // 4 - 1)
    pairs = []
    for turn in range(1, ROUTES):
        pairs += [(planes - 1, planes + turn), (planes, planes - 1 - turn)]
        if turn > 1:
            pairs += [(planes, planes + turn), (planes - 1, planes - 1 - turn)]

    barrier = pltpu.get_barrier_semaphore()
    peers = 2 + jnp.where(has_above, 1, 0) + jnp.where(has_below, 1, 0)
    for one, two in pairs:
        for here, there in ((one, two), (two, one)):
            meets = jnp.logical_and(wrapped, lat == here)
            peers = peers + jnp.where(meets, 1, 0)

            @pl.when(meets)
            def _(there=there):
                pl.semaphore_signal(barrier, inc=1, device_id={"lat": there}, device_id_type=MESH)

    @pl.when(has_above)
    def _():
        pl.semaphore_signal(barrier, inc=1, device_id=above, device_id_type=MESH)

    @pl.when(has_below)
    def _():
        pl.semaphore_signal(barrier, inc=1, device_id=below, device_id_type=MESH)

    pl.semaphore_signal(barrier, inc=1, device_id=left, device_id_type=MESH)
    pl.semaphore_signal(barrier, inc=1, device_id=right, device_id_type=MESH)

    local = [
        pltpu.make_async_copy(w_hbm, w_ref, local_sem.at[0]),
        pltpu.make_async_copy(k_hbm, k_ref, local_sem.at[1]),
        pltpu.make_async_copy(bias_hbm, bias_ref, local_sem.at[2]),
        pltpu.make_async_copy(x_hbm.at[0], own, local_sem.at[3]),
    ]
    for copy in local:
        copy.start()

    pl.semaphore_wait(barrier, peers)

    half = 2 * C

    def orient_copies(phase, chunk):
        s = lanes(chunk)
        if phase == 0:
            src, to_left, to_right = x_hbm.at[0, :, :, s], right0.at[:, :, s], left0.at[:, :, s]
        else:
            part = slice(0, half) if phase == 1 else slice(half, depth)
            src, to_left, to_right = current1.at[part, s], right1.at[part, s], left1.at[part, s]
        return (
            remote(src, to_left, left_send.at[phase, chunk], left_recv.at[phase, chunk], left),
            remote(src, to_right, right_send.at[phase, chunk], right_recv.at[phase, chunk], right),
        )

    def lat_copies(layer, chunk):
        s = lanes(chunk)
        mixed, top, bottom = ((mixed0, top0, bottom0), (mixed1, top1, bottom1))[layer]
        return (
            remote(mixed.at[0:C, s], bottom.at[:, s], up_send.at[layer, chunk], up_recv.at[layer, chunk], above),
            remote(
                mixed.at[C:half, s], top.at[:, s], down_send.at[layer, chunk], down_recv.at[layer, chunk], below
            ),
        )

    @pl.loop(0, n)
    def _(chunk):
        for copy in orient_copies(0, chunk):
            copy.start()

    @pl.when(jnp.logical_not(has_above))
    def _():
        top0[...] = jnp.zeros_like(top0)
        top1[...] = jnp.zeros_like(top1)

    @pl.when(jnp.logical_not(has_below))
    def _():
        bottom0[...] = jnp.zeros_like(bottom0)
        bottom1[...] = jnp.zeros_like(bottom1)

    for copy in local:
        copy.wait()
    build_mix0(a0, w_ref, rows)
    build_mix1(a1, w_ref)
    build_conv(c0, k_ref, cyc, 0, rows, orient, False)
    build_conv(c1, k_ref, cyc, 1, rows, orient, True)
    build_bias(b_ref, bias_ref, 0, rows, False)
    build_bias(b_ref, bias_ref, 1, rows, True)

    def mix(phase, chunk):
        s = lanes(chunk)
        if phase == 0:
            parts = [ref[:, :, s].reshape(depth, size) for ref in (left0, own, right0)]
            total = jnp.dot(a0[...], jnp.concatenate(parts, axis=0), preferred_element_type=F32)
            mixed0[:, s] = total.astype(BF)
        else:
            part = slice(0, half) if phase == 1 else slice(half, depth)
            parts = [ref[part, s] for ref in (left1, current1, right1)]
            total = jnp.dot(a1[...], jnp.concatenate(parts, axis=0), preferred_element_type=F32)
            mixed1[part, s] = total.astype(BF)

    def conv(layer, chunk):
        mixed, top, bottom, weights = ((mixed0, top0, bottom0, c0), (mixed1, top1, bottom1, c1))[layer]
        before = pl.ds(pl.multiple_of(lax.rem(chunk * size + width - edge, width), edge), edge)
        after = pl.ds(pl.multiple_of(lax.rem(chunk * size + size, width), edge), edge)

        def part(s):
            return jnp.concatenate([mixed[:, s], top[:, s], bottom[:, s]], axis=0)

        middle = part(lanes(chunk))
        wide = jnp.concatenate([part(before), middle, part(after)], axis=1)
        whole = size + 2 * edge
        west = pltpu.roll(wide, 1, 1)[:, edge : edge + size]
        east = pltpu.roll(wide, whole - 1, 1)[:, edge : edge + size]
        total = jnp.dot(weights[...], jnp.concatenate([west, middle, east], axis=0), preferred_element_type=F32)
        bias = jnp.tile(b_ref[layer], (1, size // 128))
        return jnp.maximum(total + bias, 0.0).astype(BF)

    def take(phase, chunk):
        for copy in orient_copies(phase, chunk):
            copy.wait_recv()
        mix(phase, chunk)

    def send_rows(layer, chunk):
        up, down = lat_copies(layer, chunk)
        s = lanes(chunk)
        mixed = (mixed0, mixed1)[layer]
        turn = jnp.where(wrapped, lax.rem(chunk, ROUTES), 0)
        slot = chunk // ROUTES
        via_down = jnp.logical_and(lat == planes - 1, turn != 0)
        via_up = jnp.logical_and(lat == planes, turn != 0)

        @pl.when(jnp.logical_and(has_above, jnp.logical_not(via_up)))
        def _():
            up.start()

        @pl.when(jnp.logical_and(has_below, jnp.logical_not(via_down)))
        def _():
            down.start()

        @pl.when(via_up)
        def _():
            remote(
                mixed.at[0:C, s],
                relay.at[layer, slot],
                up_send.at[layer, chunk],
                relay_recv.at[layer, slot],
                {"lat": planes - 1 - turn},
            ).start()

        @pl.when(via_down)
        def _():
            remote(
                mixed.at[C:half, s],
                relay.at[layer, slot],
                down_send.at[layer, chunk],
                relay_recv.at[layer, slot],
                {"lat": planes + turn},
            ).start()

    def relay_copies(layer, chunk):
        s = lanes(chunk)
        top, bottom = ((top0, bottom0), (top1, bottom1))[layer]
        slot = chunk // ROUTES
        held, send, came = relay.at[layer, slot], relay_send.at[layer, slot], relay_recv.at[layer, slot]
        return (
            remote(held, held, send, came, {"lat": planes}),
            remote(held, top.at[:, s], send, down_recv.at[layer, chunk], {"lat": planes}),
            remote(held, bottom.at[:, s], send, up_recv.at[layer, chunk], {"lat": planes - 1}),
        )

    def pass_rows(layer, chunk):
        turn = jnp.where(wrapped, lax.rem(chunk, ROUTES), 0)
        arrival, onward_down, onward_up = relay_copies(layer, chunk)

        @pl.when(jnp.logical_and(lat < planes - 1, turn == planes - 1 - lat))
        def _():
            arrival.wait_recv()
            onward_up.start()

        @pl.when(jnp.logical_and(lat > planes, turn == lat - planes))
        def _():
            arrival.wait_recv()
            onward_down.start()

    def take_rows(layer, chunk):
        up, down = lat_copies(layer, chunk)

        @pl.when(has_below)
        def _():
            up.wait_recv()

        @pl.when(has_above)
        def _():
            down.wait_recv()

    @pl.loop(0, n + 2 + LAG)
    def _(step):
        @pl.when(step < n)
        def _():
            take(0, step)
            send_rows(0, step)

        @pl.when(jnp.logical_and(step >= RELAY_LAG, step < n + RELAY_LAG))
        def _():
            pass_rows(0, step - RELAY_LAG)

        @pl.when(jnp.logical_and(step >= LAG, step < n + LAG))
        def _():
            take_rows(0, step - LAG)

        @pl.when(step >= LAG + 2)
        def _():
            chunk = lax.rem(step - LAG - 1, n)
            current1[:, lanes(chunk)] = conv(0, chunk)
            for copy in orient_copies(1, chunk):
                copy.start()

    @pl.loop(0, n)
    def _(step):
        for copy in orient_copies(2, lax.rem(step + 1, n)):
            copy.start()

    @pl.loop(0, n)
    def _(step):
        chunk = lax.rem(step + 1, n)
        take(1, chunk)
        send_rows(1, chunk)

        @pl.when(step >= RELAY_LAG1)
        def _():
            pass_rows(1, lax.rem(step + 1 - RELAY_LAG1, n))

    @pl.loop(0, n + 2)
    def _(step):
        @pl.when(step < RELAY_LAG1)
        def _():
            pass_rows(1, lax.rem(step + 1 + n - RELAY_LAG1, n))

        @pl.when(step < n)
        def _():
            chunk = lax.rem(step + 1, n)
            take_rows(1, chunk)
            take(2, chunk)

        @pl.when(step >= 2)
        def _():
            chunk = lax.rem(step, n)
            s = lanes(chunk)
            result[:, :, s] = conv(1, chunk).reshape(C, rows, size)
            pltpu.make_async_copy(result.at[:, :, s], out_ref.at[0, :, :, s], out_sem.at[chunk]).start()

    @pl.loop(0, n)
    def _(chunk):
        s = lanes(chunk)
        pltpu.make_async_copy(result.at[:, :, s], out_ref.at[0, :, :, s], out_sem.at[chunk]).wait()
        for phase in range(3):
            for copy in orient_copies(phase, chunk):
                copy.wait_send()
        for layer in range(LAYERS):
            up, down = lat_copies(layer, chunk)

            @pl.when(has_above)
            def _():
                up.wait_send()

            @pl.when(has_below)
            def _():
                down.wait_send()

    @pl.loop(0, n)
    def _(chunk):
        turn = jnp.where(wrapped, lax.rem(chunk, ROUTES), 0)
        passed = jnp.logical_or(
            jnp.logical_and(lat < planes - 1, turn == planes - 1 - lat),
            jnp.logical_and(lat > planes, turn == lat - planes),
        )

        @pl.when(passed)
        def _():
            for layer in range(LAYERS):
                relay_copies(layer, chunk)[0].wait_send()


def solution(mesh):
    orients, lats = mesh.shape["orient"], mesh.shape["lat"]

    def local(features, mix_weights, kernels, bias_terms):
        _, _, rows, width = features.shape
        depth = rows * C
        raw = pltpu.VMEM((C, rows, width), BF)
        flat = pltpu.VMEM((depth, width), BF)
        row = pltpu.VMEM((C, width), BF)
        sems = [pltpu.SemaphoreType.DMA((LAYERS, CHUNKS))] * 4
        slots = (CHUNKS + ROUTES - 1) // ROUTES
        slot_sems = pltpu.SemaphoreType.DMA((LAYERS, slots))
        phase_sems = [pltpu.SemaphoreType.DMA((3, CHUNKS))] * 4
        hbm = pl.BlockSpec(memory_space=pltpu.MemorySpace.HBM)
        return pl.pallas_call(
            functools.partial(kernel, orients, lats),
            out_shape=jax.ShapeDtypeStruct(features.shape, BF),
            in_specs=[hbm] * 4,
            out_specs=pl.BlockSpec(memory_space=pl.ANY),
            scratch_shapes=[raw, raw, raw, flat, flat, flat, flat, row, row, row, row, flat, raw]
            + [
                pltpu.VMEM(mix_weights.shape, BF),
                pltpu.VMEM(kernels.shape, BF),
                pltpu.VMEM(bias_terms.shape, F32),
                pltpu.VMEM((8, C, C), F32),
                pltpu.VMEM((depth, 3 * depth), BF),
                pltpu.VMEM((2 * C, 6 * C), BF),
                pltpu.VMEM((depth, 3 * (rows + 2) * C), BF),
                pltpu.VMEM((depth, 3 * (rows + 2) * C), BF),
                pltpu.VMEM((LAYERS, depth, 128), F32),
                pltpu.SemaphoreType.DMA((4,)),
            ]
            + phase_sems
            + sems
            + [pltpu.VMEM((LAYERS, slots, C, width // CHUNKS), BF), slot_sems, slot_sems]
            + [pltpu.SemaphoreType.DMA((CHUNKS,))],
            compiler_params=pltpu.CompilerParams(
                collective_id=0, has_side_effects=True, vmem_limit_bytes=40 << 20
            ),
        )(*[pltpu.with_memory_space_constraint(v, pltpu.MemorySpace.HBM) for v in (features, mix_weights, kernels, bias_terms)])

    return jax.shard_map(
        local,
        mesh=mesh,
        in_specs=(P("orient", None, "lat", None), P(), P(), P()),
        out_specs=P("orient", None, "lat", None),
        check_vma=False,
    )
```

```python
import functools

import jax
import jax.numpy as jnp
from jax import lax
from jax.experimental import pallas as pl
from jax.experimental.pallas import tpu as pltpu
from jax.sharding import PartitionSpec as P

LAYERS = 2
C = 32
MESH = pl.DeviceIdType.MESH
CHUNKS = 16
LAG = 10
RELAY_LAG = 5
RELAY_LAG1 = 8
ROUTES = 3
CYCLE_TAPS = (0, 1, 2, 5, 8, 7, 6, 3)
BF = jnp.bfloat16
F32 = jnp.float32


def iota(shape, dim):
    return lax.broadcasted_iota(jnp.int32, shape, dim)


def one_hot(cond):
    return jnp.where(cond, 1.0, 0.0).astype(BF)


def places(rows):
    order = [0, rows - 1] + list(range(1, rows - 1))
    return [order.index(r) for r in range(rows)]


def build_mix0(a_ref, w_ref, rows):
    depth = rows * C
    lane, chan = iota((C, depth), 1), iota((C, depth), 0)
    for r, at in enumerate(places(rows)):
        pick = one_hot(lane == chan * rows + r)
        for k in range(3):
            block = jnp.dot(w_ref[0, k], pick, preferred_element_type=F32)
            a_ref[at * C : (at + 1) * C, k * depth : (k + 1) * depth] = block.astype(BF)


def build_mix1(a_ref, w_ref):
    depth = 2 * C
    lane, chan = iota((C, depth), 1), iota((C, depth), 0)
    for r in range(2):
        pick = one_hot(lane == chan + r * C)
        for k in range(3):
            block = jnp.dot(w_ref[1, k], pick, preferred_element_type=F32)
            a_ref[r * C : (r + 1) * C, k * depth : (k + 1) * depth] = block.astype(BF)


def build_conv(c_ref, kern_ref, cyc_ref, layer, rows, orient, natural):
    depth = (rows + 2) * C
    at = places(rows)
    for p, tap in enumerate(CYCLE_TAPS):
        cyc_ref[p] = kern_ref[layer, tap].astype(F32)
    low = orient // 2
    high = (orient + 1) // 2
    lane, chan = iota((C, depth), 1), iota((C, depth), 0)
    for dx in range(3):
        for r in range(rows):
            total = jnp.zeros((C, depth), F32)
            for dy in range(3):
                tap = 3 * dy + dx
                if tap == 4:
                    rot = kern_ref[layer, 4]
                else:
                    p = CYCLE_TAPS.index(tap)
                    first = cyc_ref[(p + 16 - low) % 8]
                    second = cyc_ref[(p + 16 - high) % 8]
                    rot = (0.5 * first + 0.5 * second).astype(BF)
                source = r + dy - 1
                if source < 0:
                    base = rows * C
                elif source >= rows:
                    base = (rows + 1) * C
                else:
                    base = at[source] * C
                pick = one_hot(lane == chan + base)
                total = total + jnp.dot(rot, pick, preferred_element_type=F32)
            c_ref[at[r] * C : (at[r] + 1) * C, dx * depth : (dx + 1) * depth] = total.astype(BF)
    if natural:
        out, src = iota((rows * C, rows * C), 0), iota((rows * C, rows * C), 1)
        order = jnp.zeros((rows * C, rows * C), BF)
        for r in range(rows):
            order = order + one_hot((src // C == at[r]) & (out == (src % C) * rows + r))
        c_ref[...] = jnp.dot(order, c_ref[...], preferred_element_type=F32).astype(BF)


def build_bias(b_ref, bias_ref, layer, rows, natural):
    row, chan = iota((rows * C, C), 0), iota((rows * C, C), 1)
    place = row // rows if natural else row % C
    spread = jnp.where(place == chan, bias_ref[layer : layer + 1, :], 0.0)
    column = jnp.sum(spread, axis=1, keepdims=True)
    b_ref[layer] = jnp.broadcast_to(column, (rows * C, 128))


def kernel(
    orients,
    lats,
    x_hbm,
    w_hbm,
    k_hbm,
    bias_hbm,
    out_ref,
    own,
    left0,
    right0,
    left1,
    right1,
    mixed0,
    mixed1,
    top0,
    top1,
    bottom0,
    bottom1,
    current1,
    result,
    w_ref,
    k_ref,
    bias_ref,
    cyc,
    a0,
    a1,
    c0,
    c1,
    b_ref,
    local_sem,
    left_send,
    left_recv,
    right_send,
    right_recv,
    up_send,
    up_recv,
    down_send,
    down_recv,
    relay,
    relay_send,
    relay_recv,
    out_sem,
):
    rows, width = x_hbm.shape[2], x_hbm.shape[3]
    n = CHUNKS
    size = width // n
    edge = 128
    depth = rows * C
    orient = lax.axis_index("orient")
    lat = lax.axis_index("lat")
    right = {"orient": lax.rem(orient + 1, orients)}
    left = {"orient": lax.rem(orient + orients - 1, orients)}
    above = {"lat": lat - 1}
    below = {"lat": lat + 1}
    has_above = lat > 0
    has_below = lat < lats - 1

    def lanes(chunk):
        return pl.ds(pl.multiple_of(chunk * size, size), size)

    def remote(src, dst, send, recv, device):
        return pltpu.make_async_remote_copy(
            src_ref=src, dst_ref=dst, send_sem=send, recv_sem=recv, device_id=device, device_id_type=MESH
        )

    planes = lats // 2

    place = lax.rem(orient // 2, orients // 4)
    wrapped = jnp.logical_or(place == 0, place == orients // 4 - 1)
    pairs = []
    for turn in range(1, ROUTES):
        pairs += [(planes - 1, planes + turn), (planes, planes - 1 - turn)]
        if turn > 1:
            pairs += [(planes, planes + turn), (planes - 1, planes - 1 - turn)]

    barrier = pltpu.get_barrier_semaphore()
    peers = 2 + jnp.where(has_above, 1, 0) + jnp.where(has_below, 1, 0)
    for one, two in pairs:
        for here, there in ((one, two), (two, one)):
            meets = jnp.logical_and(wrapped, lat == here)
            peers = peers + jnp.where(meets, 1, 0)

            @pl.when(meets)
            def _(there=there):
                pl.semaphore_signal(barrier, inc=1, device_id={"lat": there}, device_id_type=MESH)

    @pl.when(has_above)
    def _():
        pl.semaphore_signal(barrier, inc=1, device_id=above, device_id_type=MESH)

    @pl.when(has_below)
    def _():
        pl.semaphore_signal(barrier, inc=1, device_id=below, device_id_type=MESH)

    pl.semaphore_signal(barrier, inc=1, device_id=left, device_id_type=MESH)
    pl.semaphore_signal(barrier, inc=1, device_id=right, device_id_type=MESH)

    local = [
        pltpu.make_async_copy(w_hbm, w_ref, local_sem.at[0]),
        pltpu.make_async_copy(k_hbm, k_ref, local_sem.at[1]),
        pltpu.make_async_copy(bias_hbm, bias_ref, local_sem.at[2]),
        pltpu.make_async_copy(x_hbm.at[0], own, local_sem.at[3]),
    ]
    for copy in local:
        copy.start()

    pl.semaphore_wait(barrier, peers)

    half = 2 * C

    def orient_copies(phase, chunk):
        s = lanes(chunk)
        if phase == 0:
            src, to_left, to_right = x_hbm.at[0, :, :, s], right0.at[:, :, s], left0.at[:, :, s]
        else:
            part = slice(0, half) if phase == 1 else slice(half, depth)
            src, to_left, to_right = current1.at[part, s], right1.at[part, s], left1.at[part, s]
        return (
            remote(src, to_left, left_send.at[phase, chunk], left_recv.at[phase, chunk], left),
            remote(src, to_right, right_send.at[phase, chunk], right_recv.at[phase, chunk], right),
        )

    def lat_copies(layer, chunk):
        s = lanes(chunk)
        mixed, top, bottom = ((mixed0, top0, bottom0), (mixed1, top1, bottom1))[layer]
        return (
            remote(mixed.at[0:C, s], bottom.at[:, s], up_send.at[layer, chunk], up_recv.at[layer, chunk], above),
            remote(
                mixed.at[C:half, s], top.at[:, s], down_send.at[layer, chunk], down_recv.at[layer, chunk], below
            ),
        )

    @pl.loop(0, n)
    def _(chunk):
        for copy in orient_copies(0, chunk):
            copy.start()

    @pl.when(jnp.logical_not(has_above))
    def _():
        top0[...] = jnp.zeros_like(top0)
        top1[...] = jnp.zeros_like(top1)

    @pl.when(jnp.logical_not(has_below))
    def _():
        bottom0[...] = jnp.zeros_like(bottom0)
        bottom1[...] = jnp.zeros_like(bottom1)

    for copy in local:
        copy.wait()
    build_mix0(a0, w_ref, rows)
    build_mix1(a1, w_ref)
    build_conv(c0, k_ref, cyc, 0, rows, orient, False)
    build_conv(c1, k_ref, cyc, 1, rows, orient, True)
    build_bias(b_ref, bias_ref, 0, rows, False)
    build_bias(b_ref, bias_ref, 1, rows, True)

    def mix(phase, chunk):
        s = lanes(chunk)
        if phase == 0:
            parts = [ref[:, :, s].reshape(depth, size) for ref in (left0, own, right0)]
            total = jnp.dot(a0[...], jnp.concatenate(parts, axis=0), preferred_element_type=F32)
            mixed0[:, s] = total.astype(BF)
        else:
            part = slice(0, half) if phase == 1 else slice(half, depth)
            parts = [ref[part, s] for ref in (left1, current1, right1)]
            total = jnp.dot(a1[...], jnp.concatenate(parts, axis=0), preferred_element_type=F32)
            mixed1[part, s] = total.astype(BF)

    def conv(layer, chunk):
        mixed, top, bottom, weights = ((mixed0, top0, bottom0, c0), (mixed1, top1, bottom1, c1))[layer]
        before = pl.ds(pl.multiple_of(lax.rem(chunk * size + width - edge, width), edge), edge)
        after = pl.ds(pl.multiple_of(lax.rem(chunk * size + size, width), edge), edge)

        def part(s):
            return jnp.concatenate([mixed[:, s], top[:, s], bottom[:, s]], axis=0)

        middle = part(lanes(chunk))
        wide = jnp.concatenate([part(before), middle, part(after)], axis=1)
        whole = size + 2 * edge
        west = pltpu.roll(wide, 1, 1)[:, edge : edge + size]
        east = pltpu.roll(wide, whole - 1, 1)[:, edge : edge + size]
        total = jnp.dot(weights[...], jnp.concatenate([west, middle, east], axis=0), preferred_element_type=F32)
        bias = jnp.tile(b_ref[layer], (1, size // 128))
        return jnp.maximum(total + bias, 0.0).astype(BF)

    def take(phase, chunk):
        for copy in orient_copies(phase, chunk):
            copy.wait_recv()
        mix(phase, chunk)

    def send_rows(layer, chunk):
        up, down = lat_copies(layer, chunk)
        s = lanes(chunk)
        mixed = (mixed0, mixed1)[layer]
        turn = jnp.where(wrapped, lax.rem(chunk, ROUTES), 0)
        slot = chunk // ROUTES
        via_down = jnp.logical_and(lat == planes - 1, turn != 0)
        via_up = jnp.logical_and(lat == planes, turn != 0)

        @pl.when(jnp.logical_and(has_above, jnp.logical_not(via_up)))
        def _():
            up.start()

        @pl.when(jnp.logical_and(has_below, jnp.logical_not(via_down)))
        def _():
            down.start()

        @pl.when(via_up)
        def _():
            remote(
                mixed.at[0:C, s],
                relay.at[layer, slot],
                up_send.at[layer, chunk],
                relay_recv.at[layer, slot],
                {"lat": planes - 1 - turn},
            ).start()

        @pl.when(via_down)
        def _():
            remote(
                mixed.at[C:half, s],
                relay.at[layer, slot],
                down_send.at[layer, chunk],
                relay_recv.at[layer, slot],
                {"lat": planes + turn},
            ).start()

    def relay_copies(layer, chunk):
        s = lanes(chunk)
        top, bottom = ((top0, bottom0), (top1, bottom1))[layer]
        slot = chunk // ROUTES
        held, send, came = relay.at[layer, slot], relay_send.at[layer, slot], relay_recv.at[layer, slot]
        return (
            remote(held, held, send, came, {"lat": planes}),
            remote(held, top.at[:, s], send, down_recv.at[layer, chunk], {"lat": planes}),
            remote(held, bottom.at[:, s], send, up_recv.at[layer, chunk], {"lat": planes - 1}),
        )

    def pass_rows(layer, chunk):
        turn = jnp.where(wrapped, lax.rem(chunk, ROUTES), 0)
        arrival, onward_down, onward_up = relay_copies(layer, chunk)

        @pl.when(jnp.logical_and(lat < planes - 1, turn == planes - 1 - lat))
        def _():
            arrival.wait_recv()
            onward_up.start()

        @pl.when(jnp.logical_and(lat > planes, turn == lat - planes))
        def _():
            arrival.wait_recv()
            onward_down.start()

    def take_rows(layer, chunk):
        up, down = lat_copies(layer, chunk)

        @pl.when(has_below)
        def _():
            up.wait_recv()

        @pl.when(has_above)
        def _():
            down.wait_recv()

    @pl.loop(0, n + 2 + LAG)
    def _(step):
        @pl.when(step < n)
        def _():
            take(0, step)
            send_rows(0, step)

        @pl.when(jnp.logical_and(step >= RELAY_LAG, step < n + RELAY_LAG))
        def _():
            pass_rows(0, step - RELAY_LAG)

        @pl.when(jnp.logical_and(step >= LAG, step < n + LAG))
        def _():
            take_rows(0, step - LAG)

        @pl.when(step >= LAG + 2)
        def _():
            chunk = lax.rem(step - LAG - 1, n)
            current1[:, lanes(chunk)] = conv(0, chunk)
            for copy in orient_copies(1, chunk):
                copy.start()

    @pl.loop(0, n)
    def _(step):
        for copy in orient_copies(2, lax.rem(step + 1, n)):
            copy.start()

    @pl.loop(0, n)
    def _(step):
        chunk = lax.rem(step + 1, n)
        take(1, chunk)
        send_rows(1, chunk)

        @pl.when(step >= RELAY_LAG1)
        def _():
            pass_rows(1, lax.rem(step + 1 - RELAY_LAG1, n))

    @pl.loop(0, n + 2)
    def _(step):
        @pl.when(step < RELAY_LAG1)
        def _():
            pass_rows(1, lax.rem(step + 1 + n - RELAY_LAG1, n))

        @pl.when(step < n)
        def _():
            chunk = lax.rem(step + 1, n)
            take_rows(1, chunk)
            take(2, chunk)

        @pl.when(step >= 2)
        def _():
            chunk = lax.rem(step, n)
            s = lanes(chunk)
            result[:, :, s] = conv(1, chunk).reshape(C, rows, size)
            pltpu.make_async_copy(result.at[:, :, s], out_ref.at[0, :, :, s], out_sem.at[chunk]).start()

    @pl.loop(0, n)
    def _(chunk):
        s = lanes(chunk)
        pltpu.make_async_copy(result.at[:, :, s], out_ref.at[0, :, :, s], out_sem.at[chunk]).wait()
        for phase in range(3):
            for copy in orient_copies(phase, chunk):
                copy.wait_send()
        for layer in range(LAYERS):
            up, down = lat_copies(layer, chunk)

            @pl.when(has_above)
            def _():
                up.wait_send()

            @pl.when(has_below)
            def _():
                down.wait_send()

    @pl.loop(0, n)
    def _(chunk):
        turn = jnp.where(wrapped, lax.rem(chunk, ROUTES), 0)
        passed = jnp.logical_or(
            jnp.logical_and(lat < planes - 1, turn == planes - 1 - lat),
            jnp.logical_and(lat > planes, turn == lat - planes),
        )

        @pl.when(passed)
        def _():
            for layer in range(LAYERS):
                relay_copies(layer, chunk)[0].wait_send()


def solution(mesh):
    orients, lats = mesh.shape["orient"], mesh.shape["lat"]

    def local(features, mix_weights, kernels, bias_terms):
        _, _, rows, width = features.shape
        depth = rows * C
        raw = pltpu.VMEM((C, rows, width), BF)
        flat = pltpu.VMEM((depth, width), BF)
        row = pltpu.VMEM((C, width), BF)
        sems = [pltpu.SemaphoreType.DMA((LAYERS, CHUNKS))] * 4
        slots = (CHUNKS + ROUTES - 1) // ROUTES
        slot_sems = pltpu.SemaphoreType.DMA((LAYERS, slots))
        phase_sems = [pltpu.SemaphoreType.DMA((3, CHUNKS))] * 4
        hbm = pl.BlockSpec(memory_space=pltpu.MemorySpace.HBM)
        return pl.pallas_call(
            functools.partial(kernel, orients, lats),
            out_shape=jax.ShapeDtypeStruct(features.shape, BF),
            in_specs=[hbm] * 4,
            out_specs=pl.BlockSpec(memory_space=pl.ANY),
            scratch_shapes=[raw, raw, raw, flat, flat, flat, flat, row, row, row, row, flat, raw]
            + [
                pltpu.VMEM(mix_weights.shape, BF),
                pltpu.VMEM(kernels.shape, BF),
                pltpu.VMEM(bias_terms.shape, F32),
                pltpu.VMEM((8, C, C), F32),
                pltpu.VMEM((depth, 3 * depth), BF),
                pltpu.VMEM((2 * C, 6 * C), BF),
                pltpu.VMEM((depth, 3 * (rows + 2) * C), BF),
                pltpu.VMEM((depth, 3 * (rows + 2) * C), BF),
                pltpu.VMEM((LAYERS, depth, 128), F32),
                pltpu.SemaphoreType.DMA((4,)),
            ]
            + phase_sems
            + sems
            + [pltpu.VMEM((LAYERS, slots, C, width // CHUNKS), BF), slot_sems, slot_sems]
            + [pltpu.SemaphoreType.DMA((CHUNKS,))],
            compiler_params=pltpu.CompilerParams(
                collective_id=0, has_side_effects=True, vmem_limit_bytes=40 << 20
            ),
        )(*[pltpu.with_memory_space_constraint(v, pltpu.MemorySpace.HBM) for v in (features, mix_weights, kernels, bias_terms)])

    return jax.shard_map(
        local,
        mesh=mesh,
        in_specs=(P("orient", None, "lat", None), P(), P(), P()),
        out_specs=P("orient", None, "lat", None),
        check_vma=False,
    )
```

```python
import functools

import jax
import jax.numpy as jnp
from jax import lax
from jax.experimental import pallas as pl
from jax.experimental.pallas import tpu as pltpu
from jax.sharding import PartitionSpec as P

LAYERS = 2
C = 32
MESH = pl.DeviceIdType.MESH
CHUNKS = 8
LAG = 5
RELAY_LAG = 3
RELAY_LAG1 = 4
ROUTES = 3
CYCLE_TAPS = (0, 1, 2, 5, 8, 7, 6, 3)
BF = jnp.bfloat16
F32 = jnp.float32


def iota(shape, dim):
    return lax.broadcasted_iota(jnp.int32, shape, dim)


def one_hot(cond):
    return jnp.where(cond, 1.0, 0.0).astype(BF)


def places(rows):
    order = [0, rows - 1] + list(range(1, rows - 1))
    return [order.index(r) for r in range(rows)]


def build_mix0(a_ref, w_ref, rows):
    depth = rows * C
    lane, chan = iota((C, depth), 1), iota((C, depth), 0)
    for r, at in enumerate(places(rows)):
        pick = one_hot(lane == chan * rows + r)
        for k in range(3):
            block = jnp.dot(w_ref[0, k], pick, preferred_element_type=F32)
            a_ref[at * C : (at + 1) * C, k * depth : (k + 1) * depth] = block.astype(BF)


def build_mix1(a_ref, w_ref):
    depth = 2 * C
    lane, chan = iota((C, depth), 1), iota((C, depth), 0)
    for r in range(2):
        pick = one_hot(lane == chan + r * C)
        for k in range(3):
            block = jnp.dot(w_ref[1, k], pick, preferred_element_type=F32)
            a_ref[r * C : (r + 1) * C, k * depth : (k + 1) * depth] = block.astype(BF)


def build_conv(c_ref, kern_ref, cyc_ref, layer, rows, orient, natural):
    depth = (rows + 2) * C
    at = places(rows)
    for p, tap in enumerate(CYCLE_TAPS):
        cyc_ref[p] = kern_ref[layer, tap].astype(F32)
    low = orient // 2
    high = (orient + 1) // 2
    lane, chan = iota((C, depth), 1), iota((C, depth), 0)
    for dx in range(3):
        for r in range(rows):
            total = jnp.zeros((C, depth), F32)
            for dy in range(3):
                tap = 3 * dy + dx
                if tap == 4:
                    rot = kern_ref[layer, 4]
                else:
                    p = CYCLE_TAPS.index(tap)
                    first = cyc_ref[(p + 16 - low) % 8]
                    second = cyc_ref[(p + 16 - high) % 8]
                    rot = (0.5 * first + 0.5 * second).astype(BF)
                source = r + dy - 1
                if source < 0:
                    base = rows * C
                elif source >= rows:
                    base = (rows + 1) * C
                else:
                    base = at[source] * C
                pick = one_hot(lane == chan + base)
                total = total + jnp.dot(rot, pick, preferred_element_type=F32)
            c_ref[at[r] * C : (at[r] + 1) * C, dx * depth : (dx + 1) * depth] = total.astype(BF)
    if natural:
        out, src = iota((rows * C, rows * C), 0), iota((rows * C, rows * C), 1)
        order = jnp.zeros((rows * C, rows * C), BF)
        for r in range(rows):
            order = order + one_hot((src // C == at[r]) & (out == (src % C) * rows + r))
        c_ref[...] = jnp.dot(order, c_ref[...], preferred_element_type=F32).astype(BF)


def build_bias(b_ref, bias_ref, layer, rows, natural):
    row, chan = iota((rows * C, C), 0), iota((rows * C, C), 1)
    place = row // rows if natural else row % C
    spread = jnp.where(place == chan, bias_ref[layer : layer + 1, :], 0.0)
    column = jnp.sum(spread, axis=1, keepdims=True)
    b_ref[layer] = jnp.broadcast_to(column, (rows * C, 128))


def kernel(
    orients,
    lats,
    x_hbm,
    w_hbm,
    k_hbm,
    bias_hbm,
    out_ref,
    own,
    left0,
    right0,
    left1,
    right1,
    mixed0,
    mixed1,
    top0,
    top1,
    bottom0,
    bottom1,
    current1,
    result,
    w_ref,
    k_ref,
    bias_ref,
    cyc,
    a0,
    a1,
    c0,
    c1,
    b_ref,
    local_sem,
    left_send,
    left_recv,
    right_send,
    right_recv,
    up_send,
    up_recv,
    down_send,
    down_recv,
    relay,
    relay_send,
    relay_recv,
    out_sem,
):
    rows, width = x_hbm.shape[2], x_hbm.shape[3]
    n = CHUNKS
    size = width // n
    edge = 128
    depth = rows * C
    orient = lax.axis_index("orient")
    lat = lax.axis_index("lat")
    right = {"orient": lax.rem(orient + 1, orients)}
    left = {"orient": lax.rem(orient + orients - 1, orients)}
    above = {"lat": lat - 1}
    below = {"lat": lat + 1}
    has_above = lat > 0
    has_below = lat < lats - 1

    def lanes(chunk):
        return pl.ds(pl.multiple_of(chunk * size, size), size)

    def remote(src, dst, send, recv, device):
        return pltpu.make_async_remote_copy(
            src_ref=src, dst_ref=dst, send_sem=send, recv_sem=recv, device_id=device, device_id_type=MESH
        )

    planes = lats // 2

    place = lax.rem(orient // 2, orients // 4)
    wrapped = jnp.logical_or(place == 0, place == orients // 4 - 1)
    pairs = []
    for turn in range(1, ROUTES):
        pairs += [(planes - 1, planes + turn), (planes, planes - 1 - turn)]
        if turn > 1:
            pairs += [(planes, planes + turn), (planes - 1, planes - 1 - turn)]

    barrier = pltpu.get_barrier_semaphore()
    peers = 2 + jnp.where(has_above, 1, 0) + jnp.where(has_below, 1, 0)
    for one, two in pairs:
        for here, there in ((one, two), (two, one)):
            meets = jnp.logical_and(wrapped, lat == here)
            peers = peers + jnp.where(meets, 1, 0)

            @pl.when(meets)
            def _(there=there):
                pl.semaphore_signal(barrier, inc=1, device_id={"lat": there}, device_id_type=MESH)

    @pl.when(has_above)
    def _():
        pl.semaphore_signal(barrier, inc=1, device_id=above, device_id_type=MESH)

    @pl.when(has_below)
    def _():
        pl.semaphore_signal(barrier, inc=1, device_id=below, device_id_type=MESH)

    pl.semaphore_signal(barrier, inc=1, device_id=left, device_id_type=MESH)
    pl.semaphore_signal(barrier, inc=1, device_id=right, device_id_type=MESH)

    local = [
        pltpu.make_async_copy(w_hbm, w_ref, local_sem.at[0]),
        pltpu.make_async_copy(k_hbm, k_ref, local_sem.at[1]),
        pltpu.make_async_copy(bias_hbm, bias_ref, local_sem.at[2]),
        pltpu.make_async_copy(x_hbm.at[0], own, local_sem.at[3]),
    ]
    for copy in local:
        copy.start()

    pl.semaphore_wait(barrier, peers)

    half = 2 * C

    def orient_copies(phase, chunk):
        s = lanes(chunk)
        if phase == 0:
            src, to_left, to_right = x_hbm.at[0, :, :, s], right0.at[:, :, s], left0.at[:, :, s]
        else:
            part = slice(0, half) if phase == 1 else slice(half, depth)
            src, to_left, to_right = current1.at[part, s], right1.at[part, s], left1.at[part, s]
        return (
            remote(src, to_left, left_send.at[phase, chunk], left_recv.at[phase, chunk], left),
            remote(src, to_right, right_send.at[phase, chunk], right_recv.at[phase, chunk], right),
        )

    def lat_copies(layer, chunk):
        s = lanes(chunk)
        mixed, top, bottom = ((mixed0, top0, bottom0), (mixed1, top1, bottom1))[layer]
        return (
            remote(mixed.at[0:C, s], bottom.at[:, s], up_send.at[layer, chunk], up_recv.at[layer, chunk], above),
            remote(
                mixed.at[C:half, s], top.at[:, s], down_send.at[layer, chunk], down_recv.at[layer, chunk], below
            ),
        )

    @pl.loop(0, n)
    def _(chunk):
        for copy in orient_copies(0, chunk):
            copy.start()

    @pl.when(jnp.logical_not(has_above))
    def _():
        top0[...] = jnp.zeros_like(top0)
        top1[...] = jnp.zeros_like(top1)

    @pl.when(jnp.logical_not(has_below))
    def _():
        bottom0[...] = jnp.zeros_like(bottom0)
        bottom1[...] = jnp.zeros_like(bottom1)

    for copy in local:
        copy.wait()
    build_mix0(a0, w_ref, rows)
    build_mix1(a1, w_ref)
    build_conv(c0, k_ref, cyc, 0, rows, orient, False)
    build_conv(c1, k_ref, cyc, 1, rows, orient, True)
    build_bias(b_ref, bias_ref, 0, rows, False)
    build_bias(b_ref, bias_ref, 1, rows, True)

    def mix(phase, chunk):
        s = lanes(chunk)
        if phase == 0:
            parts = [ref[:, :, s].reshape(depth, size) for ref in (left0, own, right0)]
            total = jnp.dot(a0[...], jnp.concatenate(parts, axis=0), preferred_element_type=F32)
            mixed0[:, s] = total.astype(BF)
        else:
            part = slice(0, half) if phase == 1 else slice(half, depth)
            parts = [ref[part, s] for ref in (left1, current1, right1)]
            total = jnp.dot(a1[...], jnp.concatenate(parts, axis=0), preferred_element_type=F32)
            mixed1[part, s] = total.astype(BF)

    def conv(layer, chunk):
        mixed, top, bottom, weights = ((mixed0, top0, bottom0, c0), (mixed1, top1, bottom1, c1))[layer]
        before = pl.ds(pl.multiple_of(lax.rem(chunk * size + width - edge, width), edge), edge)
        after = pl.ds(pl.multiple_of(lax.rem(chunk * size + size, width), edge), edge)

        def part(s):
            return jnp.concatenate([mixed[:, s], top[:, s], bottom[:, s]], axis=0)

        middle = part(lanes(chunk))
        wide = jnp.concatenate([part(before), middle, part(after)], axis=1)
        whole = size + 2 * edge
        west = pltpu.roll(wide, 1, 1)[:, edge : edge + size]
        east = pltpu.roll(wide, whole - 1, 1)[:, edge : edge + size]
        total = jnp.dot(weights[...], jnp.concatenate([west, middle, east], axis=0), preferred_element_type=F32)
        bias = jnp.tile(b_ref[layer], (1, size // 128))
        return jnp.maximum(total + bias, 0.0).astype(BF)

    def take(phase, chunk):
        for copy in orient_copies(phase, chunk):
            copy.wait_recv()
        mix(phase, chunk)

    def send_rows(layer, chunk):
        up, down = lat_copies(layer, chunk)
        s = lanes(chunk)
        mixed = (mixed0, mixed1)[layer]
        turn = jnp.where(wrapped, lax.rem(chunk, ROUTES), 0)
        slot = chunk // ROUTES
        via_down = jnp.logical_and(lat == planes - 1, turn != 0)
        via_up = jnp.logical_and(lat == planes, turn != 0)

        @pl.when(jnp.logical_and(has_above, jnp.logical_not(via_up)))
        def _():
            up.start()

        @pl.when(jnp.logical_and(has_below, jnp.logical_not(via_down)))
        def _():
            down.start()

        @pl.when(via_up)
        def _():
            remote(
                mixed.at[0:C, s],
                relay.at[layer, slot],
                up_send.at[layer, chunk],
                relay_recv.at[layer, slot],
                {"lat": planes - 1 - turn},
            ).start()

        @pl.when(via_down)
        def _():
            remote(
                mixed.at[C:half, s],
                relay.at[layer, slot],
                down_send.at[layer, chunk],
                relay_recv.at[layer, slot],
                {"lat": planes + turn},
            ).start()

    def relay_copies(layer, chunk):
        s = lanes(chunk)
        top, bottom = ((top0, bottom0), (top1, bottom1))[layer]
        slot = chunk // ROUTES
        held, send, came = relay.at[layer, slot], relay_send.at[layer, slot], relay_recv.at[layer, slot]
        return (
            remote(held, held, send, came, {"lat": planes}),
            remote(held, top.at[:, s], send, down_recv.at[layer, chunk], {"lat": planes}),
            remote(held, bottom.at[:, s], send, up_recv.at[layer, chunk], {"lat": planes - 1}),
        )

    def pass_rows(layer, chunk):
        turn = jnp.where(wrapped, lax.rem(chunk, ROUTES), 0)
        arrival, onward_down, onward_up = relay_copies(layer, chunk)

        @pl.when(jnp.logical_and(lat < planes - 1, turn == planes - 1 - lat))
        def _():
            arrival.wait_recv()
            onward_up.start()

        @pl.when(jnp.logical_and(lat > planes, turn == lat - planes))
        def _():
            arrival.wait_recv()
            onward_down.start()

    def take_rows(layer, chunk):
        up, down = lat_copies(layer, chunk)

        @pl.when(has_below)
        def _():
            up.wait_recv()

        @pl.when(has_above)
        def _():
            down.wait_recv()

    @pl.loop(0, n + 2 + LAG)
    def _(step):
        @pl.when(step < n)
        def _():
            take(0, step)
            send_rows(0, step)

        @pl.when(jnp.logical_and(step >= RELAY_LAG, step < n + RELAY_LAG))
        def _():
            pass_rows(0, step - RELAY_LAG)

        @pl.when(jnp.logical_and(step >= LAG, step < n + LAG))
        def _():
            take_rows(0, step - LAG)

        @pl.when(step >= LAG + 2)
        def _():
            chunk = lax.rem(step - LAG - 1, n)
            current1[:, lanes(chunk)] = conv(0, chunk)
            for copy in orient_copies(1, chunk):
                copy.start()

    @pl.loop(0, n)
    def _(step):
        for copy in orient_copies(2, lax.rem(step + 1, n)):
            copy.start()

    @pl.loop(0, n)
    def _(step):
        chunk = lax.rem(step + 1, n)
        take(1, chunk)
        send_rows(1, chunk)

        @pl.when(step >= RELAY_LAG1)
        def _():
            pass_rows(1, lax.rem(step + 1 - RELAY_LAG1, n))

    @pl.loop(0, n + 2)
    def _(step):
        @pl.when(step < RELAY_LAG1)
        def _():
            pass_rows(1, lax.rem(step + 1 + n - RELAY_LAG1, n))

        @pl.when(step < n)
        def _():
            chunk = lax.rem(step + 1, n)
            take_rows(1, chunk)
            take(2, chunk)

        @pl.when(step >= 2)
        def _():
            chunk = lax.rem(step, n)
            s = lanes(chunk)
            result[:, :, s] = conv(1, chunk).reshape(C, rows, size)
            pltpu.make_async_copy(result.at[:, :, s], out_ref.at[0, :, :, s], out_sem.at[chunk]).start()

    @pl.loop(0, n)
    def _(chunk):
        s = lanes(chunk)
        pltpu.make_async_copy(result.at[:, :, s], out_ref.at[0, :, :, s], out_sem.at[chunk]).wait()
        for phase in range(3):
            for copy in orient_copies(phase, chunk):
                copy.wait_send()
        for layer in range(LAYERS):
            up, down = lat_copies(layer, chunk)

            @pl.when(has_above)
            def _():
                up.wait_send()

            @pl.when(has_below)
            def _():
                down.wait_send()

    @pl.loop(0, n)
    def _(chunk):
        turn = jnp.where(wrapped, lax.rem(chunk, ROUTES), 0)
        passed = jnp.logical_or(
            jnp.logical_and(lat < planes - 1, turn == planes - 1 - lat),
            jnp.logical_and(lat > planes, turn == lat - planes),
        )

        @pl.when(passed)
        def _():
            for layer in range(LAYERS):
                relay_copies(layer, chunk)[0].wait_send()


def solution(mesh):
    orients, lats = mesh.shape["orient"], mesh.shape["lat"]

    def local(features, mix_weights, kernels, bias_terms):
        _, _, rows, width = features.shape
        depth = rows * C
        raw = pltpu.VMEM((C, rows, width), BF)
        flat = pltpu.VMEM((depth, width), BF)
        row = pltpu.VMEM((C, width), BF)
        sems = [pltpu.SemaphoreType.DMA((LAYERS, CHUNKS))] * 4
        slots = (CHUNKS + ROUTES - 1) // ROUTES
        slot_sems = pltpu.SemaphoreType.DMA((LAYERS, slots))
        phase_sems = [pltpu.SemaphoreType.DMA((3, CHUNKS))] * 4
        hbm = pl.BlockSpec(memory_space=pltpu.MemorySpace.HBM)
        return pl.pallas_call(
            functools.partial(kernel, orients, lats),
            out_shape=jax.ShapeDtypeStruct(features.shape, BF),
            in_specs=[hbm] * 4,
            out_specs=pl.BlockSpec(memory_space=pl.ANY),
            scratch_shapes=[raw, raw, raw, flat, flat, flat, flat, row, row, row, row, flat, raw]
            + [
                pltpu.VMEM(mix_weights.shape, BF),
                pltpu.VMEM(kernels.shape, BF),
                pltpu.VMEM(bias_terms.shape, F32),
                pltpu.VMEM((8, C, C), F32),
                pltpu.VMEM((depth, 3 * depth), BF),
                pltpu.VMEM((2 * C, 6 * C), BF),
                pltpu.VMEM((depth, 3 * (rows + 2) * C), BF),
                pltpu.VMEM((depth, 3 * (rows + 2) * C), BF),
                pltpu.VMEM((LAYERS, depth, 128), F32),
                pltpu.SemaphoreType.DMA((4,)),
            ]
            + phase_sems
            + sems
            + [pltpu.VMEM((LAYERS, slots, C, width // CHUNKS), BF), slot_sems, slot_sems]
            + [pltpu.SemaphoreType.DMA((CHUNKS,))],
            compiler_params=pltpu.CompilerParams(
                collective_id=0, has_side_effects=True, vmem_limit_bytes=40 << 20
            ),
        )(*[pltpu.with_memory_space_constraint(v, pltpu.MemorySpace.HBM) for v in (features, mix_weights, kernels, bias_terms)])

    return jax.shard_map(
        local,
        mesh=mesh,
        in_specs=(P("orient", None, "lat", None), P(), P(), P()),
        out_specs=P("orient", None, "lat", None),
        check_vma=False,
    )
```
